128 devices in a mesh: expert: 4 (over z), panel: 32 (over y, x, core).
Axes of the slice: x: 4, y: 4, z: 4, core: 2. Of those that a mesh axis runs over, the one named last changes fastest.
Arguments:
- tokens: bfloat16 [4096, 6144], P(('expert', 'panel')), may hold values from -6 to 6
- routes: int32 [4096, 2], P(('expert', 'panel')), may hold values from 0 to 7, all different within a row; in each aligned block of 32 rows (0 to 31, 32 to 63, ...) at most 12 rows name the same one
- router_weights: float32 [4096, 2], P(('expert', 'panel')), may hold values from 0.05 to 0.95
Outputs:
- hessian: float32 [8, 6144, 6144], P('expert', 'panel')
The draws below stay inside these ranges and needn't reach their ends.
Inputs may be any that keep to these rules, and one draw needn't show every extreme that they name: `routes`: each row names two different experts; among the 32 rows of one device no expert is named more than 12 times, a bound that some block reaches.
All inputs are finite; a program needn't handle non-finite values.
Results may differ from the reference program's by a relative error of at most 0.0036.
Values may be sent and summed in bfloat16 or wider, within the bound.
A program may use at most 192 MiB of HBM per device.

```python
import math
import jax
import jax.numpy as jnp
import numpy as np
from jax import lax

D = 6144
TOK_DEV = 32
CAP = 12
EXPERTS = 8
TOKENS = 4096
N_EXPERT = 4
N_PANEL = 32


def steps_of(own_key, shape, cuts, low, high):
    factor_of, own = 1.0, jax.random.fold_in(own_key, 6)
    for position, parts in cuts:
        draws = jnp.exp(jax.random.uniform(jax.random.fold_in(own, position), (parts,), jnp.float32, low / len(cuts), high / len(cuts)))
        factor_of = factor_of * jnp.repeat(draws, shape[position] // parts).reshape([-1 if axis == position else 1 for axis in range(len(shape))])
    return factor_of


def assign_block(rng, own, number, rows, amount, top, reach, lean):
    order = jax.random.permutation(rng, amount)
    packed, common = shares(amount, rows * top, reach, lean, True), shares(amount, rows * top, reach, lean, False)
    places = jnp.arange(amount)

    def named(sizes, rotation):
        used = int((sizes > 0).sum())
        fixed = max(1, used // 4)
        moved = fixed + (places - fixed + rotation * (used - fixed)) % max(1, amount - fixed)
        return jnp.zeros((amount,), jnp.int32).at[order[jnp.where(places < fixed, places, moved)]].set(jnp.asarray(sizes, jnp.int32))

    sizes = jnp.where(number % 4 == 0, named(packed, number // 4), named(common, number - number // 4 - 1))
    mixed = jax.random.permutation(jax.random.fold_in(own, 3), amount)
    giver, taker = mixed[0:amount // 2 * 2:2], mixed[1:amount // 2 * 2:2]
    margin = jnp.minimum(sizes[giver] - 1, reach - sizes[taker]) // 2
    margin = jnp.where((giver == order[0]) | (taker == order[0]) | (sizes[taker] == 0), 0, jnp.maximum(margin, 0))
    moved = jax.random.randint(jax.random.fold_in(own, 4), (amount // 2,), 0, 1 << 20) % (margin + 1)
    sizes = sizes.at[giver].add(-moved).at[taker].add(moved)
    labels = jnp.searchsorted(jnp.cumsum(sizes), jnp.arange(rows * top), side="right").astype(jnp.int32)
    table = labels.reshape(top, rows).T
    table = table[jax.random.permutation(jax.random.fold_in(own, 1), rows)]
    rotation = jax.random.randint(jax.random.fold_in(own, 2), (rows, 1), 0, top)
    return jnp.take_along_axis(table, (jnp.arange(top)[None, :] + rotation) % top, axis=1)


def shares(amount, total, bound, lean, full):
    loads = [(1 << 20) // math.isqrt(grade ** lean) + 1 for grade in range(1, amount + 1)]
    largest = bound if full else min(bound, max(-(-total // amount), total * loads[0] // sum(loads)))
    least = 1 if total - largest >= amount - 1 else 0
    holding, surplus = [largest] + [least] * (amount - 1), total - largest - least * (amount - 1)
    while surplus > 0:
        free = [i for i in range(1, amount) if holding[i] < largest] or [i for i in range(1, amount) if holding[i] < bound]
        pool, left = sum([loads[i] for i in free]), surplus
        for i in free:
            more = min(bound - holding[i], max(1, left * loads[i] // pool), surplus)
            holding[i] = holding[i] + more
            surplus = surplus - more
    return np.array(holding)


def scatter_about(own_key, shape, deviation, bound, split=(), kind=jnp.bfloat16):
    entries = deviation * jax.random.normal(own_key, shape, jnp.float32)
    if split:
        entries = entries * steps_of(own_key, shape, split, -0.22, 0.18)
    return jnp.clip(entries, -bound, bound).astype(kind)


def setup_inputs(seed: int = 0) -> dict:
    seeds = jax.random.split(jax.random.key(seed), 4)
    tokens = scatter_about(seeds[0], (TOKENS, D), 1.0, 6.0, ((0, 128),))
    routes_keys = jax.random.split(jax.random.fold_in(seeds[1], 1), TOKENS // TOK_DEV)
    routes_turns = jax.random.permutation(jax.random.fold_in(seeds[1], 3), TOKENS // TOK_DEV)
    routes = jax.vmap(lambda own, number: assign_block(jax.random.fold_in(seeds[1], 2), own, number, TOK_DEV, EXPERTS, 2, CAP, 2))(routes_keys, routes_turns).reshape((TOKENS, 2))
    router_weights = jnp.clip(0.05 + 0.9 * jax.random.uniform(seeds[2], (TOKENS, 2), jnp.float32) ** steps_of(seeds[2], (TOKENS, 2), ((0, 128),), -0.2, 0.2), 0.05, 0.95)
    return dict(tokens=tokens, routes=routes, router_weights=router_weights)


def place_of(routes):
    blocks = routes.reshape(N_EXPERT * N_PANEL, TOK_DEV * 2)
    onehot = (blocks[:, :, None] == jnp.arange(EXPERTS, dtype=jnp.int32)).astype(jnp.int32)
    before = jnp.cumsum(onehot, axis=1) - onehot
    slots = jnp.sum(onehot * before, axis=2)
    device = jnp.arange(N_EXPERT * N_PANEL, dtype=jnp.int32)[:, None]
    return (device * CAP + slots).astype(jnp.int32).reshape(TOKENS, 2)


def reference(tokens, routes, router_weights):
    places = place_of(routes)
    rounded = lax.optimization_barrier(router_weights.astype(jnp.bfloat16)).astype(jnp.float32)
    widened = tokens.astype(jnp.float32)
    slot_total = N_EXPERT * N_PANEL * CAP
    scaling = float(slot_total) ** -0.5

    def one_expert(expert):
        chosen = routes == expert
        picked = jnp.any(chosen, axis=1)
        index = jnp.where(picked, jnp.sum(jnp.where(chosen, places, 0), axis=1), slot_total).astype(jnp.int32)
        factor = jnp.sum(jnp.where(chosen, rounded, 0.0), axis=1)
        scaled = lax.optimization_barrier((factor[:, None] * widened).astype(jnp.bfloat16)).astype(jnp.float32)
        plain = jnp.zeros((slot_total, D), jnp.float32).at[index].set(widened, mode="drop")
        weighted = jnp.zeros((slot_total, D), jnp.float32).at[index].set(scaled, mode="drop")
        return jnp.dot(plain.T, weighted, precision=lax.Precision.HIGHEST) * scaling

    return lax.map(one_expert, jnp.arange(EXPERTS, dtype=jnp.int32))
```

```python
import jax
import jax.numpy as jnp
from jax import lax
from jax.sharding import PartitionSpec as P

EXPERTS = 8
CAP = 12


def per_device(tokens, routes, router_weights):
    count, width = tokens.shape
    groups = lax.axis_size("expert")
    panels = lax.axis_size("panel")
    quarter = width // groups
    panel_width = width // panels
    scaling = float(groups * panels * CAP) ** (-0.5)
    rounded = router_weights.astype(jnp.bfloat16)
    ids = jnp.arange(64, dtype=jnp.int32)[None, :]
    zero = jnp.zeros((), jnp.bfloat16)
    dense = jnp.where(routes[:, 0:1] == ids, rounded[:, 0:1], zero) + jnp.where(
        routes[:, 1:2] == ids, rounded[:, 1:2], zero
    )
    seed = lax.all_to_all(
        tokens.reshape(count, groups, quarter), "expert", split_axis=1, concat_axis=0, tiled=True
    ).reshape(groups * count, quarter)
    columns = lax.all_gather(seed, "panel", axis=0, tiled=True)
    rows = jnp.concatenate(
        [
            tokens.reshape(count, panels, panel_width),
            jnp.broadcast_to(dense[:, None, :], (count, panels, 64)),
        ],
        axis=2,
    )
    rows = lax.all_to_all(rows, "panel", split_axis=1, concat_axis=0, tiled=True)
    rows = rows.reshape(panels * count, panel_width + 64)
    rows = lax.all_gather(rows, "expert", axis=0, tiled=True)
    rows = rows.reshape(groups, panels, count, panel_width + 64).transpose(3, 1, 0, 2)
    rows = rows.reshape(panel_width + 64, -1)
    weights = rows[panel_width : panel_width + EXPERTS]
    scaled = (weights[:, None, :] * rows[None, :panel_width, :]).reshape(-1, rows.shape[1])
    blocks = jnp.dot(scaled, columns, preferred_element_type=jnp.float32) * scaling
    blocks = blocks.astype(jnp.bfloat16).reshape(groups, EXPERTS // groups, panel_width, quarter)
    blocks = lax.all_to_all(blocks, "expert", split_axis=0, concat_axis=0, tiled=True)
    return blocks.transpose(1, 2, 0, 3).reshape(-1, panel_width, width).astype(jnp.float32)


def solution(mesh):
    placed = (
        P(("expert", "panel"), None),
        P(("expert", "panel"), None),
        P(("expert", "panel"), None),
    )
    return jax.shard_map(
        per_device,
        mesh=mesh,
        in_specs=placed,
        out_specs=P("expert", "panel", None),
        check_vma=False,
    )
```

```python
import jax
import jax.numpy as jnp
from jax import lax
from jax.experimental import pallas as pl
from jax.experimental.pallas import tpu as pltpu
from jax.sharding import PartitionSpec as P

MESH = pl.DeviceIdType.MESH
Z, Y, X, C = 4, 4, 4, 2
EXPERTS = 8
OWN = EXPERTS // Z
CAP = 12
TOK = 32
WPAD = 128
TILE = 256
PIECES = ((0, 640), (640, 512), (1152, 512))
PLANE = [(dy, dx) for dy in range(Y) for dx in range(X) if (dy, dx) != (0, 0)]


def kernel(
    tok, routes, router_weights, out,
    cols, rows, rows_t, scaled, stage,
    own_sem, x1_s, x1_r, x2_s, x2_r, xd_s, xd_r, seed_s, seed_r,
    p1_s, p1_r, p2_s, p2_r, d_s, d_r, out_s, out_r, keep_sem,
):
    width = tok.shape[1]
    quarter = width // Z
    chip_rows = width // (Y * X)
    dev_rows = chip_rows // C
    scaling = float(Z * Y * X * C * CAP) ** -0.5
    z = lax.axis_index("expert")
    p = lax.axis_index("panel")
    y, x, c = p // (X * C), lax.rem(p // C, X), lax.rem(p, C)

    def at_z(dz):
        return (lax.rem(z + dz, Z), p)

    def at_plane(dy, dx):
        return (z, (lax.rem(y + dy, Y) * X + lax.rem(x + dx, X)) * C + c)

    sibling = (z, p + 1 - 2 * c)

    def remote(src, dst, send, recv, device):
        return pltpu.make_async_remote_copy(
            src_ref=src, dst_ref=dst, send_sem=send, recv_sem=recv, device_id=device, device_id_type=MESH
        )

    ids = lax.broadcasted_iota(jnp.int32, (TOK, WPAD), 1)
    chosen = routes[...]
    rounded = router_weights[...].astype(jnp.bfloat16).astype(jnp.float32)
    dense = jnp.where(ids == chosen[:, 0:1], rounded[:, 0:1], 0.0) + jnp.where(
        ids == chosen[:, 1:2], rounded[:, 1:2], 0.0
    )
    cols[z, y, x, c, :, 0:WPAD] = dense.astype(jnp.bfloat16)

    barrier = pltpu.get_barrier_semaphore()
    peers = [at_z(dz) for dz in range(1, Z)] + [at_plane(dy, dx) for dy, dx in PLANE] + [sibling]
    for peer in peers:
        pl.semaphore_signal(barrier, inc=1, device_id=peer, device_id_type=MESH)
    pl.semaphore_wait(barrier, len(peers))

    def own_columns(device_z, start, size):
        return pl.ds(pl.multiple_of(device_z * quarter + start, 128), size)

    def row_columns(chip):
        return pl.ds(pl.multiple_of(chip * chip_rows, 128), chip_rows)

    x1 = []
    for k, (dy, dx) in enumerate(PLANE):
        chip = lax.rem(y + dy, Y) * X + lax.rem(x + dx, X)
        x1.append(
            remote(tok.at[:, row_columns(chip)], rows.at[z, y, x, c], x1_s.at[k], x1_r.at[k], at_plane(dy, dx))
        )
    x2 = [
        remote(rows.at[z, :, :, c], rows.at[z, :, :, c], x2_s.at[k], x2_r.at[k], at_z(k + 1)) for k in range(Z - 1)
    ]
    xd = remote(rows.at[:, :, :, c], rows.at[:, :, :, c], xd_s, xd_r, sibling)
    seeds = []
    for q, (low, size) in enumerate(PIECES):
        start = max(low, WPAD)
        span = low + size - start
        here = []
        for k in range(Z - 1):
            there = at_z(k + 1)
            here.append(
                remote(
                    tok.at[:, own_columns(there[0], start - WPAD, span)],
                    cols.at[z, y, x, c, :, pl.ds(start, span)],
                    seed_s.at[q, k], seed_r.at[q, k], there,
                )
            )
        seeds.append(here)
    weight_seeds = [
        remote(
            cols.at[z, y, x, c, :, pl.ds(0, WPAD)], cols.at[z, y, x, c, :, pl.ds(0, WPAD)],
            seed_s.at[len(PIECES), k], seed_r.at[len(PIECES), k], at_z(k + 1),
        )
        for k in range(Z - 1)
    ]
    seeds[0] = seeds[0] + weight_seeds
    p1, p2, d = [], [], []
    for q, (low, size) in enumerate(PIECES):
        span = pl.ds(low, size)
        first, second = [], []
        for k in range(3):
            along_x, along_y = at_plane(0, k + 1), at_plane(k + 1, 0)
            a1 = cols.at[pl.ds(0, 2), y, x, c, :, span]
            b1 = cols.at[pl.ds(2, 2), y, x, c, :, span]
            first.append(remote(a1, a1, p1_s.at[q, 0, k], p1_r.at[q, 0, k], along_x))
            first.append(remote(b1, b1, p1_s.at[q, 1, k], p1_r.at[q, 1, k], along_y))
            a2 = cols.at[pl.ds(0, 2), y, :, c, :, span]
            b2 = cols.at[pl.ds(2, 2), :, x, c, :, span]
            second.append(remote(a2, a2, p2_s.at[q, 0, k], p2_r.at[q, 0, k], along_y))
            second.append(remote(b2, b2, p2_s.at[q, 1, k], p2_r.at[q, 1, k], along_x))
        p1.append(first)
        p2.append(second)
        both = cols.at[:, :, :, c, :, span]
        d.append(remote(both, both, d_s.at[q], d_r.at[q], sibling))

    own_rows = pltpu.make_async_copy(tok.at[:, row_columns(y * X + x)], rows.at[z, y, x, c], own_sem.at[0])
    own_cols = pltpu.make_async_copy(
        tok.at[:, own_columns(z, 0, quarter)], cols.at[z, y, x, c, :, pl.ds(WPAD, quarter)], own_sem.at[1]
    )
    own_rows.start()
    own_cols.start()
    for copy in x1:
        copy.start()
    for here in seeds:
        for copy in here:
            copy.start()
    own_cols.wait()
    own_rows.wait()
    for q in range(len(PIECES)):
        for copy in seeds[q]:
            copy.wait_recv()
        for copy in p1[q]:
            copy.start()
    for copy in x1:
        copy.wait_recv()
    for copy in x2:
        copy.start()
    for q in range(len(PIECES)):
        for copy in p1[q]:
            copy.wait_recv()
        for copy in p2[q]:
            copy.start()
    for copy in p2[0]:
        copy.wait_recv()
    d[0].start()
    for copy in x2:
        copy.wait_recv()
    xd.start()
    d[0].wait_recv()
    xd.wait_recv()

    def build(j, carry):
        z0, y0 = j // Y, lax.rem(j, Y)
        span = pl.ds(pl.multiple_of(j * 256, 256), 256)
        rows_t[...] = rows[z0, y0].reshape(256, chip_rows).astype(jnp.float32).T
        weights = cols[z0, y0, :, :, :, 0:WPAD].reshape(256, WPAD).astype(jnp.float32).T
        own = rows_t[pl.ds(pl.multiple_of(c * dev_rows, dev_rows), dev_rows), :]
        for e in range(EXPERTS):
            scaled[pl.ds(e * dev_rows, dev_rows), span] = (own * weights[e : e + 1, :]).astype(jnp.bfloat16)
        return carry

    lax.fori_loop(0, Z * Y, build, 0)

    sent, kept = [], []
    tile = 0
    for q, (low, size) in enumerate(PIECES):
        start = max(low, WPAD)
        for lane in range(start, low + size, TILE):
            if lane == start and q > 0:
                d[q].wait_recv()
            place = lane - WPAD
            for k in (2, 1, 3, 0):
                owner = lax.rem(z + k, Z)
                total = jnp.zeros((OWN * dev_rows, TILE), jnp.float32)
                for z0 in range(Z):
                    left = scaled[
                        pl.ds(pl.multiple_of(owner * OWN * dev_rows, OWN * dev_rows), OWN * dev_rows),
                        pl.ds(z0 * 1024, 1024),
                    ]
                    right = cols[z0, :, :, :, :, pl.ds(lane, TILE)].reshape(1024, TILE)
                    total = total + jnp.dot(left, right, preferred_element_type=jnp.float32)
                stage[owner, :, :, pl.ds(place, TILE)] = (
                    (total * scaling).astype(jnp.bfloat16).reshape(OWN, dev_rows, TILE)
                )
                source = stage.at[owner, :, :, pl.ds(place, TILE)]
                target = out.at[:, :, own_columns(z, place, TILE)]
                if k:
                    copy = remote(source, target, out_s.at[tile, k - 1], out_r.at[tile, k - 1], at_z(k))
                    sent.append(copy)
                else:
                    copy = pltpu.make_async_copy(source, target, keep_sem.at[tile])
                    kept.append(copy)
                copy.start()
            if lane == start and q + 1 < len(PIECES):
                for copy in p2[q + 1]:
                    copy.wait_recv()
                d[q + 1].start()
            tile += 1

    for copy in kept:
        copy.wait()
    for copy in sent:
        copy.wait_recv()
    done = x1 + x2 + [xd] + [copy for group in seeds + p1 + p2 for copy in group] + d + sent
    for copy in done:
        copy.wait_send()


def per_device(tokens, routes, router_weights):
    width = tokens.shape[1]
    quarter = width // Z
    chip_rows = width // (Y * X)
    dev_rows = chip_rows // C
    count = Z * Y * X * C * TOK
    pieces = len(PIECES)
    dma = pltpu.SemaphoreType.DMA
    blocks = pl.pallas_call(
        kernel,
        out_shape=jax.ShapeDtypeStruct((OWN, dev_rows, width), jnp.bfloat16),
        in_specs=[pl.BlockSpec(memory_space=pltpu.VMEM)] * 3,
        out_specs=pl.BlockSpec(memory_space=pl.ANY),
        scratch_shapes=[
            pltpu.VMEM((Z, Y, X, C, TOK, WPAD + quarter), jnp.bfloat16),
            pltpu.VMEM((Z, Y, X, C, TOK, chip_rows), jnp.bfloat16),
            pltpu.VMEM((chip_rows, 256), jnp.float32),
            pltpu.VMEM((EXPERTS * dev_rows, count), jnp.bfloat16),
            pltpu.VMEM((Z, OWN, dev_rows, quarter), jnp.bfloat16),
            dma((2,)),
            dma((len(PLANE),)), dma((len(PLANE),)),
            dma((Z - 1,)), dma((Z - 1,)),
            dma, dma,
            dma((pieces + 1, Z - 1)), dma((pieces + 1, Z - 1)),
            dma((pieces, 2, 3)), dma((pieces, 2, 3)),
            dma((pieces, 2, 3)), dma((pieces, 2, 3)),
            dma((pieces,)), dma((pieces,)),
            dma((quarter // TILE, Z - 1)), dma((quarter // TILE, Z - 1)),
            dma((quarter // TILE,)),
        ],
        compiler_params=pltpu.CompilerParams(
            collective_id=0, has_side_effects=True, vmem_limit_bytes=56 << 20
        ),
    )(tokens, routes, router_weights)
    return blocks.astype(jnp.float32)


def solution(mesh):
    placed = (
        P(("expert", "panel"), None),
        P(("expert", "panel"), None),
        P(("expert", "panel"), None),
    )
    return jax.shard_map(
        per_device,
        mesh=mesh,
        in_specs=placed,
        out_specs=P("expert", "panel", None),
        check_vma=False,
    )
```

```python
import jax
import jax.numpy as jnp
from jax import lax
from jax.experimental import pallas as pl
from jax.experimental.pallas import tpu as pltpu
from jax.sharding import PartitionSpec as P

MESH = pl.DeviceIdType.MESH
Z, Y, X, C = 4, 4, 4, 2
EXPERTS = 8
OWN = EXPERTS // Z
CAP = 12
TOK = 32
WPAD = 128
TILE = 256
COMMON = 1024
PIECES = ((0, 384), (384, 512), (896, 512), (1408, 512), (1920, 512))
PLANE = [(dy, dx) for dy in range(Y) for dx in range(X) if (dy, dx) != (0, 0)]
COPIES = 160
LOCALS = 16


def kernel(tok, routes, router_weights, out, cols, rows, rows_t, scaled, stage, mine, send, recv, local):
    width = tok.shape[1]
    part = (width - COMMON) // Z
    chip_rows = width // (Y * X)
    dev_rows = chip_rows // C
    scaling = float(Z * Y * X * C * CAP) ** -0.5
    z = lax.axis_index("expert")
    p = lax.axis_index("panel")
    y, x, c = p // (X * C), lax.rem(p // C, X), lax.rem(p, C)
    up_z, down_z = lax.rem(z + 1, Z), lax.rem(z + 3, Z)
    up_y, down_y = lax.rem(y + 1, Y), lax.rem(y + 3, Y)
    up_x, down_x = lax.rem(x + 1, X), lax.rem(x + 3, X)

    def at_z(dz):
        return (lax.rem(z + dz, Z), p)

    def at_plane(dy, dx):
        return (z, (lax.rem(y + dy, Y) * X + lax.rem(x + dx, X)) * C + c)

    sibling = (z, p + 1 - 2 * c)
    started, kept = [], []

    def push(src, dst, device):
        k = len(started)
        copy = pltpu.make_async_remote_copy(
            src_ref=src, dst_ref=dst, send_sem=send.at[k], recv_sem=recv.at[k], device_id=device, device_id_type=MESH
        )
        copy.start()
        started.append(copy)
        return copy

    def same(ref, device):
        return push(ref, ref, device)

    def keep(src, dst):
        copy = pltpu.make_async_copy(src, dst, local.at[len(kept)])
        copy.start()
        kept.append(copy)
        return copy

    def arrive(copies):
        for copy in copies:
            copy.wait_recv()

    ids = lax.broadcasted_iota(jnp.int32, (WPAD, TOK), 0)
    chosen = routes[...]
    rounded = router_weights[...].astype(jnp.bfloat16).astype(jnp.float32)
    dense = jnp.where(ids == chosen[0:1, :], rounded[0:1, :], 0.0) + jnp.where(
        ids == chosen[1:2, :], rounded[1:2, :], 0.0
    )
    cols[z, y, x, c, :, 0:WPAD] = dense.T.astype(jnp.bfloat16)

    barrier = pltpu.get_barrier_semaphore()
    peers = [at_z(dz) for dz in range(1, Z)] + [at_plane(dy, dx) for dy, dx in PLANE] + [sibling]
    for peer in peers:
        pl.semaphore_signal(barrier, inc=1, device_id=peer, device_id_type=MESH)
    pl.semaphore_wait(barrier, len(peers))

    def part_columns(device_z, start, size):
        return pl.ds(pl.multiple_of(COMMON + device_z * part + start, 128), size)

    def row_columns(chip):
        return pl.ds(pl.multiple_of(chip * chip_rows, 128), chip_rows)

    x1 = []
    for dy, dx in PLANE:
        chip = lax.rem(y + dy, Y) * X + lax.rem(x + dx, X)
        x1.append(push(tok.at[:, row_columns(chip)], rows.at[z, y, x, c], at_plane(dy, dx)))
    seeds = []
    for q, (low, size) in enumerate(PIECES):
        here = []
        start = max(low, WPAD)
        span = low + size - start
        for k in (1, 3, 2):
            there = at_z(k)
            if q == 0:
                here.append(same(cols.at[z, y, x, c, :, pl.ds(0, WPAD)], there))
            if start < WPAD + part:
                source = tok.at[:, part_columns(there[0], start - WPAD, span)]
            else:
                source = tok.at[:, pl.ds(start - WPAD - part, span)]
            here.append(push(source, cols.at[z, y, x, c, :, pl.ds(start, span)], there))
        seeds.append(here)
    keep(tok.at[:, row_columns(y * X + x)], rows.at[z, y, x, c])
    keep(tok.at[:, part_columns(z, 0, part)], cols.at[z, y, x, c, :, pl.ds(WPAD, part)])
    keep(tok.at[:, pl.ds(0, COMMON)], cols.at[z, y, x, c, :, pl.ds(WPAD + part, COMMON)])
    for copy in kept:
        copy.wait()
    kept_before = len(kept)

    p1, p2, f2, d = {}, {}, {}, {}

    def span_of(q):
        return pl.ds(*PIECES[q])

    def phase1(q):
        arrive(seeds[q])
        s = span_of(q)
        p1[q] = []
        for k in (1, 3, 2):
            p1[q].append(same(cols.at[pl.ds(0, 2), y, x, c, :, s], at_plane(0, k)))
            p1[q].append(same(cols.at[pl.ds(2, 2), y, x, c, :, s], at_plane(k, 0)))

    def phase2(q):
        arrive(p1[q])
        s = span_of(q)
        p2[q] = []
        for k in (1, 3):
            p2[q].append(same(cols.at[pl.ds(0, 2), y, :, c, :, s], at_plane(k, 0)))
            p2[q].append(same(cols.at[pl.ds(2, 2), :, x, c, :, s], at_plane(0, k)))

    def forward(q):
        arrive(p2[q])
        s = span_of(q)
        f2[q] = [
            same(cols.at[0, down_y, :, c, :, s], at_plane(1, 0)),
            same(cols.at[2, :, down_x, c, :, s], at_plane(0, 1)),
            same(cols.at[1, up_y, :, c, :, s], at_plane(3, 0)),
            same(cols.at[3, :, up_x, c, :, s], at_plane(0, 3)),
        ]

    def share(q):
        arrive(f2[q])
        d[q] = same(cols.at[:, :, :, c, :, span_of(q)], sibling)

    def half(block, h):
        return rows.at[block, pl.ds(2 * h, 2), :, c]

    phase1(0)
    phase1(1)
    arrive(x1)
    up = [same(half(z, 0), at_z(1)), same(half(z, 1), at_z(1))]
    down = [same(half(z, 1), at_z(3)), same(half(z, 0), at_z(3))]
    xd = [same(rows.at[z, :, :, c], sibling)]
    phase2(0)
    phase1(2)
    arrive([up[0], down[0]])
    far = [same(half(down_z, 0), at_z(1)), same(half(up_z, 1), at_z(3))]
    forward(0)
    phase2(1)
    arrive([up[1]])
    xd.append(same(rows.at[down_z, :, :, c], sibling))
    arrive([down[1]])
    xd.append(same(rows.at[up_z, :, :, c], sibling))
    phase1(3)
    share(0)
    forward(1)
    arrive(far)
    xd.append(same(rows.at[lax.rem(z + 2, Z), :, :, c], sibling))
    phase2(2)
    phase1(4)
    d[0].wait_recv()

    def build(z0, y0, carry):
        span = pl.ds(pl.multiple_of((z0 * Y + y0) * 256, 256), 256)
        rows_t[...] = rows[z0, y0].reshape(256, chip_rows).astype(jnp.float32).T
        weights = cols[z0, y0, :, :, :, 0:WPAD].reshape(256, WPAD).astype(jnp.float32).T
        own = rows_t[pl.ds(pl.multiple_of(c * dev_rows, dev_rows), dev_rows), :]
        for e in range(EXPERTS):
            scaled[pl.ds(e * dev_rows, dev_rows), span] = (own * weights[e : e + 1, :]).astype(jnp.bfloat16)
        return carry

    for k, block in enumerate((z, down_z, up_z, lax.rem(z + 2, Z))):
        xd[k].wait_recv()
        lax.fori_loop(0, Y, lambda y0, carry, block=block: build(block, y0, carry), 0)

    def product(owner, lane):
        total = jnp.zeros((OWN * dev_rows, TILE), jnp.float32)
        first = pl.multiple_of(owner * OWN * dev_rows, OWN * dev_rows)
        for z0 in range(Z):
            left = scaled[pl.ds(first, OWN * dev_rows), pl.ds(z0 * 1024, 1024)]
            right = cols[z0, :, :, :, :, pl.ds(lane, TILE)].reshape(1024, TILE)
            total = total + jnp.dot(left, right, preferred_element_type=jnp.float32)
        return (total * scaling).astype(jnp.bfloat16).reshape(OWN, dev_rows, TILE)

    tiles = []

    def split_tile(lane):
        place = lane - WPAD
        for k in (2, 1, 3, 0):
            owner = lax.rem(z + k, Z)
            stage[owner, :, :, pl.ds(place, TILE)] = product(owner, lane)
            source = stage.at[owner, :, :, pl.ds(place, TILE)]
            target = out.at[:, :, part_columns(z, place, TILE)]
            if k:
                tiles.append(push(source, target, at_z(k)))
            else:
                keep(source, target)

    def common_tile(lane):
        place = lane - WPAD - part
        mine[:, :, pl.ds(place, TILE)] = product(z, lane)
        keep(mine.at[:, :, pl.ds(place, TILE)], out.at[:, :, pl.ds(place, TILE)])

    split_tile(128)
    share(1)
    forward(2)
    phase2(3)
    d[1].wait_recv()
    split_tile(384)
    phase2(4)
    split_tile(640)
    share(2)
    forward(3)
    d[2].wait_recv()
    split_tile(896)
    share(3)
    forward(4)
    split_tile(1152)
    d[3].wait_recv()
    common_tile(1408)
    common_tile(1664)
    share(4)
    d[4].wait_recv()
    common_tile(1920)
    common_tile(2176)

    for copy in kept[kept_before:]:
        copy.wait()
    arrive(tiles)
    for copy in started:
        copy.wait_send()


def per_device(tokens, routes, router_weights):
    width = tokens.shape[1]
    part = (width - COMMON) // Z
    chip_rows = width // (Y * X)
    dev_rows = chip_rows // C
    count = Z * Y * X * C * TOK
    dma = pltpu.SemaphoreType.DMA
    blocks = pl.pallas_call(
        kernel,
        out_shape=jax.ShapeDtypeStruct((OWN, dev_rows, width), jnp.bfloat16),
        in_specs=[pl.BlockSpec(memory_space=pltpu.VMEM)] * 3,
        out_specs=pl.BlockSpec(memory_space=pl.ANY),
        scratch_shapes=[
            pltpu.VMEM((Z, Y, X, C, TOK, WPAD + part + COMMON), jnp.bfloat16),
            pltpu.VMEM((Z, Y, X, C, TOK, chip_rows), jnp.bfloat16),
            pltpu.VMEM((chip_rows, 256), jnp.float32),
            pltpu.VMEM((EXPERTS * dev_rows, count), jnp.bfloat16),
            pltpu.VMEM((Z, OWN, dev_rows, part), jnp.bfloat16),
            pltpu.VMEM((OWN, dev_rows, COMMON), jnp.bfloat16),
            dma((COPIES,)),
            dma((COPIES,)),
            dma((LOCALS,)),
        ],
        compiler_params=pltpu.CompilerParams(
            collective_id=0, has_side_effects=True, vmem_limit_bytes=56 << 20
        ),
    )(tokens, routes.T, router_weights.T)
    return blocks.astype(jnp.float32)


def solution(mesh):
    placed = (
        P(("expert", "panel"), None),
        P(("expert", "panel"), None),
        P(("expert", "panel"), None),
    )
    return jax.shard_map(
        per_device,
        mesh=mesh,
        in_specs=placed,
        out_specs=P("expert", "panel", None),
        check_vma=False,
    )
```

```python
import jax
import jax.numpy as jnp
from jax import lax
from jax.experimental import pallas as pl
from jax.experimental.pallas import tpu as pltpu
from jax.sharding import PartitionSpec as P

MESH = pl.DeviceIdType.MESH
Z, Y, X, C = 4, 4, 4, 2
EXPERTS = 8
OWN = EXPERTS // Z
CAP = 12
TOK = 32
WPAD = 128
TILE = 256
FAR = 512
PIECES = ((0, 384), (384, 512), (896, 512), (1408, 256), (1664, 512))
PLANE = [(dy, dx) for dy in range(Y) for dx in range(X) if (dy, dx) != (0, 0)]
COPIES = 160
LOCALS = 4
STRIP = 16


def kernel(tok, routes, router_weights, out, cols, rows, rows_t, scaled, stage, send, recv, local):
    width = tok.shape[1]
    part = width // Z
    chip_rows = width // (Y * X)
    dev_rows = chip_rows // C
    scaling = float(Z * Y * X * C * CAP) ** -0.5
    z = lax.axis_index("expert")
    p = lax.axis_index("panel")
    y, x, c = p // (X * C), lax.rem(p // C, X), lax.rem(p, C)
    up_z, down_z = lax.rem(z + 1, Z), lax.rem(z + 3, Z)

    def at_z(dz):
        return (lax.rem(z + dz, Z), p)

    def at_plane(dy, dx):
        return (z, (lax.rem(y + dy, Y) * X + lax.rem(x + dx, X)) * C + c)

    sibling = (z, p + 1 - 2 * c)
    started, kept = [], []

    def push(src, dst, device):
        k = len(started)
        copy = pltpu.make_async_remote_copy(
            src_ref=src, dst_ref=dst, send_sem=send.at[k], recv_sem=recv.at[k], device_id=device, device_id_type=MESH
        )
        copy.start()
        started.append(copy)
        return copy

    def same(ref, device):
        return push(ref, ref, device)

    def keep(src, dst):
        copy = pltpu.make_async_copy(src, dst, local.at[len(kept)])
        copy.start()
        kept.append(copy)
        return copy

    def arrive(copies):
        for copy in copies:
            copy.wait_recv()

    ids = lax.broadcasted_iota(jnp.int32, (WPAD, TOK), 0)
    chosen = routes[...]
    rounded = router_weights[...].astype(jnp.bfloat16).astype(jnp.float32)
    dense = jnp.where(ids == chosen[0:1, :], rounded[0:1, :], 0.0) + jnp.where(
        ids == chosen[1:2, :], rounded[1:2, :], 0.0
    )
    cols[z, y, x, c, :, 0:WPAD] = dense.T.astype(jnp.bfloat16)

    barrier = pltpu.get_barrier_semaphore()
    peers = [at_z(dz) for dz in range(1, Z)] + [at_plane(dy, dx) for dy, dx in PLANE] + [sibling]
    for peer in peers:
        pl.semaphore_signal(barrier, inc=1, device_id=peer, device_id_type=MESH)
    pl.semaphore_wait(barrier, len(peers))

    def part_columns(device_z, start, size):
        return pl.ds(pl.multiple_of(device_z * part + start, 128), size)

    def far_columns(device_z, start, size):
        return part_columns(lax.rem(device_z + 2, Z), part - FAR + start, size)

    def row_columns(chip):
        return pl.ds(pl.multiple_of(chip * chip_rows, 128), chip_rows)

    def seed(q):
        here = []
        low, size = PIECES[q]
        start = max(low, WPAD)
        span = low + size - start
        for k in (1, 3, 2):
            there = at_z(k)
            if q == 0:
                here.append(same(cols.at[z, y, x, c, :, pl.ds(0, WPAD)], there))
            if start < WPAD + part:
                source = tok.at[:, part_columns(there[0], start - WPAD, span)]
            else:
                source = tok.at[:, far_columns(there[0], start - WPAD - part, span)]
            here.append(push(source, cols.at[z, y, x, c, :, pl.ds(start, span)], there))
        return here

    seeds = [seed(0)]
    x1 = []
    for dy, dx in PLANE:
        chip = lax.rem(y + dy, Y) * X + lax.rem(x + dx, X)
        x1.append(push(tok.at[:, row_columns(chip)], rows.at[z, y, x, c], at_plane(dy, dx)))
    seeds += [seed(q) for q in range(1, len(PIECES))]
    keep(tok.at[:, row_columns(y * X + x)], rows.at[z, y, x, c])
    keep(tok.at[:, part_columns(z, 0, part)], cols.at[z, y, x, c, :, pl.ds(WPAD, part)])
    keep(tok.at[:, far_columns(z, 0, FAR)], cols.at[z, y, x, c, :, pl.ds(WPAD + part, FAR)])
    for copy in kept:
        copy.wait()

    p1, p2, d = {}, {}, {}

    def span_of(q):
        return pl.ds(*PIECES[q])

    def phase1(q):
        arrive(seeds[q])
        s = span_of(q)
        p1[q] = []
        for k in (1, 3, 2):
            p1[q].append(same(cols.at[pl.ds(0, 2), y, x, c, :, s], at_plane(0, k)))
            p1[q].append(same(cols.at[pl.ds(2, 2), y, x, c, :, s], at_plane(k, 0)))

    def phase2(q):
        arrive(p1[q])
        s = span_of(q)
        p2[q] = []
        for k in (1, 3, 2):
            p2[q].append(same(cols.at[pl.ds(0, 2), y, :, c, :, s], at_plane(k, 0)))
            p2[q].append(same(cols.at[pl.ds(2, 2), :, x, c, :, s], at_plane(0, k)))

    def share(q):
        arrive(p2[q])
        d[q] = same(cols.at[:, :, :, c, :, span_of(q)], sibling)

    def half(block, h):
        return rows.at[block, pl.ds(2 * h, 2), :, c]

    phase1(0)
    arrive(x1)
    up = [same(half(z, 0), at_z(1)), same(half(z, 1), at_z(1))]
    down = [same(half(z, 1), at_z(3)), same(half(z, 0), at_z(3))]
    xd = [same(rows.at[z, :, :, c], sibling)]
    phase1(1)
    phase2(0)
    phase1(2)
    arrive([up[0], down[0]])
    far = [same(half(down_z, 0), at_z(1)), same(half(up_z, 1), at_z(3))]
    phase2(1)
    arrive([up[1]])
    xd.append(same(rows.at[down_z, :, :, c], sibling))
    arrive([down[1]])
    xd.append(same(rows.at[up_z, :, :, c], sibling))
    phase1(3)
    share(0)
    phase2(2)
    arrive(far)
    xd.append(same(rows.at[lax.rem(z + 2, Z), :, :, c], sibling))
    phase1(4)
    d[0].wait_recv()

    def build(z0, y0, carry):
        span = pl.ds(pl.multiple_of((z0 * Y + y0) * 256, 256), 256)
        rows_t[...] = rows[z0, y0].reshape(256, chip_rows).astype(jnp.float32).T
        weights = cols[z0, y0, :, :, :, 0:WPAD].reshape(256, WPAD).astype(jnp.float32).T
        own = rows_t[pl.ds(pl.multiple_of(c * dev_rows, dev_rows), dev_rows), :]
        for e in range(EXPERTS):
            scaled[pl.ds(e * dev_rows, dev_rows), span] = (own * weights[e : e + 1, :]).astype(jnp.bfloat16)
        return carry

    for k, block in enumerate((z, down_z, up_z, lax.rem(z + 2, Z))):
        xd[k].wait_recv()
        lax.fori_loop(0, Y, lambda y0, carry, block=block: build(block, y0, carry), 0)

    def product(owner, lane):
        total = jnp.zeros((OWN * dev_rows, TILE), jnp.float32)
        first = pl.multiple_of(owner * OWN * dev_rows, OWN * dev_rows)
        for z0 in range(Z):
            left = scaled[pl.ds(first, OWN * dev_rows), pl.ds(z0 * 1024, 1024)]
            right = cols[z0, :, :, :, :, pl.ds(lane, TILE)].reshape(1024, TILE)
            total = total + jnp.dot(left, right, preferred_element_type=jnp.float32)
        return (total * scaling).astype(jnp.bfloat16).reshape(OWN, dev_rows, TILE)

    tiles = []

    def split_tile(lane, between):
        place = lane - WPAD
        for k in (2, 1, 3, 0):
            if k == 2 and place >= part - FAR:
                continue
            owner = lax.rem(z + k, Z)
            target = part_columns(z, place, TILE)
            if k:
                source = stage.at[k - 1, :, :, pl.ds(place, TILE)]
                source[...] = product(owner, lane)
                tiles.append(push(source, out.at[:, :, target], at_z(k)))
            else:
                out[:, :, target] = product(owner, lane)
            for step, q in between.get(k, ()):
                step(q)

    def far_tile(lane):
        place = lane - WPAD - part
        out[:, :, far_columns(z, place, TILE)] = product(z, lane)

    split_tile(128, {0: ((share, 1), (phase2, 3))})
    d[1].wait_recv()
    split_tile(384, {})
    split_tile(640, {1: ((share, 2), (phase2, 4))})
    d[2].wait_recv()
    split_tile(896, {0: ((share, 3),)})
    split_tile(1152, {})
    d[3].wait_recv()
    split_tile(1408, {})
    share(4)
    d[4].wait_recv()
    far_tile(1664)
    far_tile(1920)

    arrive(tiles)
    for copy in started:
        copy.wait_send()


def widen(blocks, out, wide, sem):
    dev_rows = blocks.shape[1]
    copies = []
    for k in range(OWN * dev_rows // STRIP):
        e, low = k * STRIP // dev_rows, k * STRIP % dev_rows
        wide[k] = blocks[e, low : low + STRIP, :].astype(jnp.float32)
        copies.append(pltpu.make_async_copy(wide.at[k], out.at[e, pl.ds(low, STRIP), :], sem.at[k]))
        copies[-1].start()
    for copy in copies:
        copy.wait()


def per_device(tokens, routes, router_weights):
    width = tokens.shape[1]
    part = width // Z
    chip_rows = width // (Y * X)
    dev_rows = chip_rows // C
    count = Z * Y * X * C * TOK
    dma = pltpu.SemaphoreType.DMA
    blocks = pl.pallas_call(
        kernel,
        out_shape=pltpu.VMEM((OWN, dev_rows, width), jnp.bfloat16),
        in_specs=[pl.BlockSpec(memory_space=pltpu.VMEM)] * 3,
        out_specs=pl.BlockSpec(memory_space=pltpu.VMEM),
        scratch_shapes=[
            pltpu.VMEM((Z, Y, X, C, TOK, WPAD + part + FAR), jnp.bfloat16),
            pltpu.VMEM((Z, Y, X, C, TOK, chip_rows), jnp.bfloat16),
            pltpu.VMEM((chip_rows, 256), jnp.float32),
            pltpu.VMEM((EXPERTS * dev_rows, count), jnp.bfloat16),
            pltpu.VMEM((Z - 1, OWN, dev_rows, part), jnp.bfloat16),
            dma((COPIES,)),
            dma((COPIES,)),
            dma((LOCALS,)),
        ],
        compiler_params=pltpu.CompilerParams(
            collective_id=0, has_side_effects=True, vmem_limit_bytes=50 << 20
        ),
    )(tokens, routes.T, router_weights.T)
    return pl.pallas_call(
        widen,
        out_shape=jax.ShapeDtypeStruct((OWN, dev_rows, width), jnp.float32),
        in_specs=[pl.BlockSpec(memory_space=pltpu.VMEM)],
        out_specs=pl.BlockSpec(memory_space=pl.ANY),
        scratch_shapes=[pltpu.VMEM((OWN * dev_rows // STRIP, STRIP, width), jnp.float32), dma((OWN * dev_rows // STRIP,))],
        compiler_params=pltpu.CompilerParams(vmem_limit_bytes=16 << 20),
    )(blocks)


def solution(mesh):
    placed = (
        P(("expert", "panel"), None),
        P(("expert", "panel"), None),
        P(("expert", "panel"), None),
    )
    return jax.shard_map(
        per_device,
        mesh=mesh,
        in_specs=placed,
        out_specs=P("expert", "panel", None),
        check_vma=False,
    )
```

```python
import jax
import jax.numpy as jnp
from jax import lax
from jax.experimental import pallas as pl
from jax.experimental.pallas import tpu as pltpu
from jax.sharding import PartitionSpec as P

MESH = pl.DeviceIdType.MESH
Z, Y, X, C = 4, 4, 4, 2
EXPERTS = 8
OWN = EXPERTS // Z
CAP = 12
TOK = 32
WPAD = 128
TILE = 256
FAR = 512
PIECES = ((0, 384), (384, 512), (896, 512), (1408, 256), (1664, 512))
PLANE = [(dy, dx) for dy in range(Y) for dx in range(X) if (dy, dx) != (0, 0)]
COPIES = 160
LOCALS = 4
STRIP = 16


def kernel(tok, routes, router_weights, out, cols, rows, rows_t, scaled, stage, send, recv, local):
    width = tok.shape[1]
    part = width // Z
    chip_rows = width // (Y * X)
    dev_rows = chip_rows // C
    scaling = float(Z * Y * X * C * CAP) ** -0.5
    z = lax.axis_index("expert")
    p = lax.axis_index("panel")
    y, x, c = p // (X * C), lax.rem(p // C, X), lax.rem(p, C)
    up_z, down_z = lax.rem(z + 1, Z), lax.rem(z + 3, Z)

    def at_z(dz):
        return (lax.rem(z + dz, Z), p)

    def at_plane(dy, dx):
        return (z, (lax.rem(y + dy, Y) * X + lax.rem(x + dx, X)) * C + c)

    sibling = (z, p + 1 - 2 * c)
    started, kept = [], []

    def push(src, dst, device):
        k = len(started)
        copy = pltpu.make_async_remote_copy(
            src_ref=src, dst_ref=dst, send_sem=send.at[k], recv_sem=recv.at[k], device_id=device, device_id_type=MESH
        )
        copy.start()
        started.append(copy)
        return copy

    def same(ref, device):
        return push(ref, ref, device)

    def keep(src, dst):
        copy = pltpu.make_async_copy(src, dst, local.at[len(kept)])
        copy.start()
        kept.append(copy)
        return copy

    def arrive(copies):
        for copy in copies:
            copy.wait_recv()

    ids = lax.broadcasted_iota(jnp.int32, (WPAD, TOK), 0)
    chosen = routes[...]
    rounded = router_weights[...].astype(jnp.bfloat16).astype(jnp.float32)
    dense = jnp.where(ids == chosen[0:1, :], rounded[0:1, :], 0.0) + jnp.where(
        ids == chosen[1:2, :], rounded[1:2, :], 0.0
    )
    cols[z, y, x, c, :, 0:WPAD] = dense.T.astype(jnp.bfloat16)

    barrier = pltpu.get_barrier_semaphore()
    peers = [at_z(dz) for dz in range(1, Z)] + [at_plane(dy, dx) for dy, dx in PLANE] + [sibling]
    for peer in peers:
        pl.semaphore_signal(barrier, inc=1, device_id=peer, device_id_type=MESH)
    pl.semaphore_wait(barrier, len(peers))

    def part_columns(device_z, start, size):
        return pl.ds(pl.multiple_of(device_z * part + start, 128), size)

    def far_columns(device_z, start, size):
        return part_columns(lax.rem(device_z + 2, Z), part - FAR + start, size)

    def row_columns(chip):
        return pl.ds(pl.multiple_of(chip * chip_rows, 128), chip_rows)

    def seed(q):
        here = []
        low, size = PIECES[q]
        start = max(low, WPAD)
        span = low + size - start
        for k in (1, 3, 2):
            there = at_z(k)
            if q == 0:
                here.append(same(cols.at[z, y, x, c, :, pl.ds(0, WPAD)], there))
            if start < WPAD + part:
                source = tok.at[:, part_columns(there[0], start - WPAD, span)]
            else:
                source = tok.at[:, far_columns(there[0], start - WPAD - part, span)]
            here.append(push(source, cols.at[z, y, x, c, :, pl.ds(start, span)], there))
        return here

    seeds = [seed(0)]
    x1 = []
    for dy, dx in PLANE:
        chip = lax.rem(y + dy, Y) * X + lax.rem(x + dx, X)
        x1.append(push(tok.at[:, row_columns(chip)], rows.at[z, y, x, c], at_plane(dy, dx)))
    seeds += [seed(q) for q in range(1, len(PIECES))]
    keep(tok.at[:, row_columns(y * X + x)], rows.at[z, y, x, c])
    keep(tok.at[:, part_columns(z, 0, part)], cols.at[z, y, x, c, :, pl.ds(WPAD, part)])
    keep(tok.at[:, far_columns(z, 0, FAR)], cols.at[z, y, x, c, :, pl.ds(WPAD + part, FAR)])
    for copy in kept:
        copy.wait()

    p1, p2, d = {}, {}, {}

    def span_of(q):
        return pl.ds(*PIECES[q])

    def phase1(q):
        arrive(seeds[q])
        s = span_of(q)
        p1[q] = []
        for k in (1, 3, 2):
            p1[q].append(same(cols.at[pl.ds(0, 2), y, x, c, :, s], at_plane(0, k)))
            p1[q].append(same(cols.at[pl.ds(2, 2), y, x, c, :, s], at_plane(k, 0)))

    def phase2(q):
        arrive(p1[q])
        s = span_of(q)
        p2[q] = []
        for k in (1, 3, 2):
            p2[q].append(same(cols.at[pl.ds(0, 2), y, :, c, :, s], at_plane(k, 0)))
            p2[q].append(same(cols.at[pl.ds(2, 2), :, x, c, :, s], at_plane(0, k)))

    def share(q):
        arrive(p2[q])
        d[q] = same(cols.at[:, :, :, c, :, span_of(q)], sibling)

    def half(block, h):
        return rows.at[block, pl.ds(2 * h, 2), :, c]

    phase1(0)
    arrive(x1)
    up = [same(half(z, 0), at_z(1)), same(half(z, 1), at_z(1))]
    down = [same(half(z, 1), at_z(3)), same(half(z, 0), at_z(3))]
    xd = [same(rows.at[z, :, :, c], sibling)]
    phase1(1)
    phase2(0)
    phase1(2)
    arrive([up[0], down[0]])
    far = [same(half(down_z, 0), at_z(1)), same(half(up_z, 1), at_z(3))]
    phase2(1)
    arrive([up[1]])
    xd.append(same(rows.at[down_z, :, :, c], sibling))
    arrive([down[1]])
    xd.append(same(rows.at[up_z, :, :, c], sibling))
    phase1(3)
    share(0)
    phase2(2)
    arrive(far)
    xd.append(same(rows.at[lax.rem(z + 2, Z), :, :, c], sibling))
    phase1(4)
    d[0].wait_recv()

    def build(z0, y0, carry):
        span = pl.ds(pl.multiple_of((z0 * Y + y0) * 256, 256), 256)
        rows_t[...] = rows[z0, y0].reshape(256, chip_rows).astype(jnp.float32).T
        weights = cols[z0, y0, :, :, :, 0:WPAD].reshape(256, WPAD).astype(jnp.float32).T
        own = rows_t[pl.ds(pl.multiple_of(c * dev_rows, dev_rows), dev_rows), :]
        for e in range(EXPERTS):
            scaled[pl.ds(e * dev_rows, dev_rows), span] = (own * weights[e : e + 1, :]).astype(jnp.bfloat16)
        return carry

    for k, block in enumerate((z, down_z, up_z, lax.rem(z + 2, Z))):
        xd[k].wait_recv()
        lax.fori_loop(0, Y, lambda y0, carry, block=block: build(block, y0, carry), 0)

    def product(owner, lane):
        total = jnp.zeros((OWN * dev_rows, TILE), jnp.float32)
        first = pl.multiple_of(owner * OWN * dev_rows, OWN * dev_rows)
        for z0 in range(Z):
            left = scaled[pl.ds(first, OWN * dev_rows), pl.ds(z0 * 1024, 1024)]
            right = cols[z0, :, :, :, :, pl.ds(lane, TILE)].reshape(1024, TILE)
            total = total + jnp.dot(left, right, preferred_element_type=jnp.float32)
        return (total * scaling).astype(jnp.bfloat16).reshape(OWN, dev_rows, TILE)

    tiles = []

    def split_tile(lane, between, which=(2, 1, 3, 0)):
        place = lane - WPAD
        for k in which:
            if k == 2 and place >= part - FAR:
                continue
            owner = lax.rem(z + k, Z)
            target = part_columns(z, place, TILE)
            if k:
                source = stage.at[k - 1, :, :, pl.ds(place, TILE)]
                source[...] = product(owner, lane)
                tiles.append(push(source, out.at[:, :, target], at_z(k)))
            else:
                out[:, :, target] = product(owner, lane)
            for step, q in between.get(k, ()):
                step(q)

    def far_tile(lane):
        place = lane - WPAD - part
        out[:, :, far_columns(z, place, TILE)] = product(z, lane)

    split_tile(128, {3: ((share, 1), (phase2, 3))}, (2, 1, 3))
    d[1].wait_recv()
    split_tile(384, {}, (2, 1, 3))
    split_tile(640, {1: ((share, 2), (phase2, 4))}, (2, 1, 3))
    split_tile(128, {}, (0,))
    d[2].wait_recv()
    split_tile(896, {3: ((share, 3),)}, (2, 1, 3))
    split_tile(1152, {}, (2, 1, 3))
    split_tile(384, {}, (0,))
    d[3].wait_recv()
    split_tile(1408, {}, (2, 1, 3))
    share(4)
    for lane in (640, 896, 1152, 1408):
        split_tile(lane, {}, (0,))
    d[4].wait_recv()
    far_tile(1664)
    far_tile(1920)

    arrive(tiles)
    for copy in started:
        copy.wait_send()


def widen(blocks, out, wide, sem):
    dev_rows = blocks.shape[1]
    copies = []
    for k in range(OWN * dev_rows // STRIP):
        e, low = k * STRIP // dev_rows, k * STRIP % dev_rows
        wide[k] = blocks[e, low : low + STRIP, :].astype(jnp.float32)
        copies.append(pltpu.make_async_copy(wide.at[k], out.at[e, pl.ds(low, STRIP), :], sem.at[k]))
        copies[-1].start()
    for copy in copies:
        copy.wait()


def per_device(tokens, routes, router_weights):
    width = tokens.shape[1]
    part = width // Z
    chip_rows = width // (Y * X)
    dev_rows = chip_rows // C
    count = Z * Y * X * C * TOK
    dma = pltpu.SemaphoreType.DMA
    blocks = pl.pallas_call(
        kernel,
        out_shape=pltpu.VMEM((OWN, dev_rows, width), jnp.bfloat16),
        in_specs=[pl.BlockSpec(memory_space=pltpu.VMEM)] * 3,
        out_specs=pl.BlockSpec(memory_space=pltpu.VMEM),
        scratch_shapes=[
            pltpu.VMEM((Z, Y, X, C, TOK, WPAD + part + FAR), jnp.bfloat16),
            pltpu.VMEM((Z, Y, X, C, TOK, chip_rows), jnp.bfloat16),
            pltpu.VMEM((chip_rows, 256), jnp.float32),
            pltpu.VMEM((EXPERTS * dev_rows, count), jnp.bfloat16),
            pltpu.VMEM((Z - 1, OWN, dev_rows, part), jnp.bfloat16),
            dma((COPIES,)),
            dma((COPIES,)),
            dma((LOCALS,)),
        ],
        compiler_params=pltpu.CompilerParams(
            collective_id=0, has_side_effects=True, vmem_limit_bytes=50 << 20
        ),
    )(tokens, routes.T, router_weights.T)
    return pl.pallas_call(
        widen,
        out_shape=jax.ShapeDtypeStruct((OWN, dev_rows, width), jnp.float32),
        in_specs=[pl.BlockSpec(memory_space=pltpu.VMEM)],
        out_specs=pl.BlockSpec(memory_space=pl.ANY),
        scratch_shapes=[pltpu.VMEM((OWN * dev_rows // STRIP, STRIP, width), jnp.float32), dma((OWN * dev_rows // STRIP,))],
        compiler_params=pltpu.CompilerParams(vmem_limit_bytes=16 << 20),
    )(blocks)


def solution(mesh):
    placed = (
        P(("expert", "panel"), None),
        P(("expert", "panel"), None),
        P(("expert", "panel"), None),
    )
    return jax.shard_map(
        per_device,
        mesh=mesh,
        in_specs=placed,
        out_specs=P("expert", "panel", None),
        check_vma=False,
    )
```

```python
import jax
import jax.numpy as jnp
from jax import lax
from jax.experimental import pallas as pl
from jax.experimental.pallas import tpu as pltpu
from jax.sharding import PartitionSpec as P

MESH = pl.DeviceIdType.MESH
Z, Y, X, C = 4, 4, 4, 2
EXPERTS = 8
OWN = EXPERTS // Z
CAP = 12
TOK = 32
WPAD = 128
TILE = 256
FAR = 512
PIECES = ((0, 384), (384, 512), (896, 512), (1408, 256), (1664, 512))
PLANE = [(dy, dx) for dy in range(Y) for dx in range(X) if (dy, dx) != (0, 0)]
COPIES = 160
LOCALS = 4
STRIP = 16


def kernel(tok, routes, router_weights, out, cols, rows, rows_t, scaled, stage, send, recv, local):
    width = tok.shape[1]
    part = width // Z
    chip_rows = width // (Y * X)
    dev_rows = chip_rows // C
    scaling = float(Z * Y * X * C * CAP) ** -0.5
    z = lax.axis_index("expert")
    p = lax.axis_index("panel")
    y, x, c = p // (X * C), lax.rem(p // C, X), lax.rem(p, C)
    up_z, down_z = lax.rem(z + 1, Z), lax.rem(z + 3, Z)

    def at_z(dz):
        return (lax.rem(z + dz, Z), p)

    def at_plane(dy, dx):
        return (z, (lax.rem(y + dy, Y) * X + lax.rem(x + dx, X)) * C + c)

    sibling = (z, p + 1 - 2 * c)
    started, kept = [], []

    def push(src, dst, device):
        k = len(started)
        copy = pltpu.make_async_remote_copy(
            src_ref=src, dst_ref=dst, send_sem=send.at[k], recv_sem=recv.at[k], device_id=device, device_id_type=MESH
        )
        copy.start()
        started.append(copy)
        return copy

    def same(ref, device):
        return push(ref, ref, device)

    def keep(src, dst):
        copy = pltpu.make_async_copy(src, dst, local.at[len(kept)])
        copy.start()
        kept.append(copy)
        return copy

    def arrive(copies):
        for copy in copies:
            copy.wait_recv()

    ids = lax.broadcasted_iota(jnp.int32, (WPAD, TOK), 0)
    chosen = routes[...]
    rounded = router_weights[...].astype(jnp.bfloat16).astype(jnp.float32)
    dense = jnp.where(ids == chosen[0:1, :], rounded[0:1, :], 0.0) + jnp.where(
        ids == chosen[1:2, :], rounded[1:2, :], 0.0
    )
    cols[z, y, x, c, :, 0:WPAD] = dense.T.astype(jnp.bfloat16)

    barrier = pltpu.get_barrier_semaphore()
    peers = [at_z(dz) for dz in range(1, Z)] + [at_plane(dy, dx) for dy, dx in PLANE] + [sibling]
    for peer in peers:
        pl.semaphore_signal(barrier, inc=1, device_id=peer, device_id_type=MESH)
    pl.semaphore_wait(barrier, len(peers))

    def part_columns(device_z, start, size):
        return pl.ds(pl.multiple_of(device_z * part + start, 128), size)

    def far_columns(device_z, start, size):
        return part_columns(lax.rem(device_z + 2, Z), part - FAR + start, size)

    def row_columns(chip):
        return pl.ds(pl.multiple_of(chip * chip_rows, 128), chip_rows)

    def seed(q):
        here = []
        low, size = PIECES[q]
        start = max(low, WPAD)
        span = low + size - start
        for k in (1, 3, 2):
            there = at_z(k)
            if q == 0:
                here.append(same(cols.at[z, y, x, c, :, pl.ds(0, WPAD)], there))
            if start < WPAD + part:
                source = tok.at[:, part_columns(there[0], start - WPAD, span)]
            else:
                source = tok.at[:, far_columns(there[0], start - WPAD - part, span)]
            here.append(push(source, cols.at[z, y, x, c, :, pl.ds(start, span)], there))
        return here

    x1 = []
    for dy, dx in PLANE:
        chip = lax.rem(y + dy, Y) * X + lax.rem(x + dx, X)
        x1.append(push(tok.at[:, row_columns(chip)], rows.at[z, y, x, c], at_plane(dy, dx)))
    seeds = [seed(0)]
    seeds += [seed(q) for q in range(1, len(PIECES))]
    keep(tok.at[:, row_columns(y * X + x)], rows.at[z, y, x, c])
    keep(tok.at[:, part_columns(z, 0, part)], cols.at[z, y, x, c, :, pl.ds(WPAD, part)])
    keep(tok.at[:, far_columns(z, 0, FAR)], cols.at[z, y, x, c, :, pl.ds(WPAD + part, FAR)])
    for copy in kept:
        copy.wait()

    p1, p2, d = {}, {}, {}

    def span_of(q):
        return pl.ds(*PIECES[q])

    def phase1(q):
        arrive(seeds[q])
        s = span_of(q)
        p1[q] = []
        for k in (1, 3, 2):
            p1[q].append(same(cols.at[pl.ds(0, 2), y, x, c, :, s], at_plane(0, k)))
            p1[q].append(same(cols.at[pl.ds(2, 2), y, x, c, :, s], at_plane(k, 0)))

    def phase2(q):
        arrive(p1[q])
        s = span_of(q)
        p2[q] = []
        for k in (1, 3, 2):
            p2[q].append(same(cols.at[pl.ds(0, 2), y, :, c, :, s], at_plane(k, 0)))
            p2[q].append(same(cols.at[pl.ds(2, 2), :, x, c, :, s], at_plane(0, k)))

    def share(q):
        arrive(p2[q])
        d[q] = same(cols.at[:, :, :, c, :, span_of(q)], sibling)

    def half(block, h):
        return rows.at[block, pl.ds(2 * h, 2), :, c]

    phase1(0)
    arrive(x1)
    up = [same(half(z, 0), at_z(1)), same(half(z, 1), at_z(1))]
    down = [same(half(z, 1), at_z(3)), same(half(z, 0), at_z(3))]
    xd = [same(rows.at[z, :, :, c], sibling)]
    phase1(1)
    phase2(0)
    phase1(2)
    arrive([up[0], down[0]])
    far = [same(half(down_z, 0), at_z(1)), same(half(up_z, 1), at_z(3))]
    phase2(1)
    arrive([up[1]])
    xd.append(same(rows.at[down_z, :, :, c], sibling))
    arrive([down[1]])
    xd.append(same(rows.at[up_z, :, :, c], sibling))
    phase1(3)
    share(0)
    phase2(2)
    arrive(far)
    xd.append(same(rows.at[lax.rem(z + 2, Z), :, :, c], sibling))
    phase1(4)
    d[0].wait_recv()

    def build(z0, y0, carry):
        span = pl.ds(pl.multiple_of((z0 * Y + y0) * 256, 256), 256)
        rows_t[...] = rows[z0, y0].reshape(256, chip_rows).astype(jnp.float32).T
        weights = cols[z0, y0, :, :, :, 0:WPAD].reshape(256, WPAD).astype(jnp.float32).T
        own = rows_t[pl.ds(pl.multiple_of(c * dev_rows, dev_rows), dev_rows), :]
        for e in range(EXPERTS):
            scaled[pl.ds(e * dev_rows, dev_rows), span] = (own * weights[e : e + 1, :]).astype(jnp.bfloat16)
        return carry

    for k, block in enumerate((z, down_z, up_z, lax.rem(z + 2, Z))):
        xd[k].wait_recv()
        lax.fori_loop(0, Y, lambda y0, carry, block=block: build(block, y0, carry), 0)

    def product(owner, lane):
        total = jnp.zeros((OWN * dev_rows, TILE), jnp.float32)
        first = pl.multiple_of(owner * OWN * dev_rows, OWN * dev_rows)
        for z0 in range(Z):
            left = scaled[pl.ds(first, OWN * dev_rows), pl.ds(z0 * 1024, 1024)]
            right = cols[z0, :, :, :, :, pl.ds(lane, TILE)].reshape(1024, TILE)
            total = total + jnp.dot(left, right, preferred_element_type=jnp.float32)
        return (total * scaling).astype(jnp.bfloat16).reshape(OWN, dev_rows, TILE)

    tiles = []

    def split_tile(lane, between, which=(2, 1, 3, 0)):
        place = lane - WPAD
        for k in which:
            if k == 2 and place >= part - FAR:
                continue
            owner = lax.rem(z + k, Z)
            target = part_columns(z, place, TILE)
            if k:
                source = stage.at[k - 1, :, :, pl.ds(place, TILE)]
                source[...] = product(owner, lane)
                tiles.append(push(source, out.at[:, :, target], at_z(k)))
            else:
                out[:, :, target] = product(owner, lane)
            for step, q in between.get(k, ()):
                step(q)

    def far_tile(lane):
        place = lane - WPAD - part
        out[:, :, far_columns(z, place, TILE)] = product(z, lane)

    split_tile(128, {3: ((share, 1), (phase2, 3))}, (2, 1, 3))
    d[1].wait_recv()
    split_tile(384, {}, (2, 1, 3))
    split_tile(640, {1: ((share, 2), (phase2, 4))}, (2, 1, 3))
    split_tile(128, {}, (0,))
    d[2].wait_recv()
    split_tile(896, {3: ((share, 3),)}, (2, 1, 3))
    split_tile(1152, {}, (2, 1, 3))
    split_tile(384, {}, (0,))
    d[3].wait_recv()
    split_tile(1408, {}, (2, 1, 3))
    share(4)
    for lane in (640, 896, 1152, 1408):
        split_tile(lane, {}, (0,))
    d[4].wait_recv()
    far_tile(1664)
    far_tile(1920)

    arrive(tiles)
    for copy in started:
        copy.wait_send()


def widen(blocks, out, wide, sem):
    dev_rows = blocks.shape[1]
    copies = []
    for k in range(OWN * dev_rows // STRIP):
        e, low = k * STRIP // dev_rows, k * STRIP % dev_rows
        wide[k] = blocks[e, low : low + STRIP, :].astype(jnp.float32)
        copies.append(pltpu.make_async_copy(wide.at[k], out.at[e, pl.ds(low, STRIP), :], sem.at[k]))
        copies[-1].start()
    for copy in copies:
        copy.wait()


def per_device(tokens, routes, router_weights):
    width = tokens.shape[1]
    part = width // Z
    chip_rows = width // (Y * X)
    dev_rows = chip_rows // C
    count = Z * Y * X * C * TOK
    dma = pltpu.SemaphoreType.DMA
    blocks = pl.pallas_call(
        kernel,
        out_shape=pltpu.VMEM((OWN, dev_rows, width), jnp.bfloat16),
        in_specs=[pl.BlockSpec(memory_space=pl.ANY)] + [pl.BlockSpec(memory_space=pltpu.VMEM)] * 2,
        out_specs=pl.BlockSpec(memory_space=pltpu.VMEM),
        scratch_shapes=[
            pltpu.VMEM((Z, Y, X, C, TOK, WPAD + part + FAR), jnp.bfloat16),
            pltpu.VMEM((Z, Y, X, C, TOK, chip_rows), jnp.bfloat16),
            pltpu.VMEM((chip_rows, 256), jnp.float32),
            pltpu.VMEM((EXPERTS * dev_rows, count), jnp.bfloat16),
            pltpu.VMEM((Z - 1, OWN, dev_rows, part), jnp.bfloat16),
            dma((COPIES,)),
            dma((COPIES,)),
            dma((LOCALS,)),
        ],
        compiler_params=pltpu.CompilerParams(
            collective_id=0, has_side_effects=True, vmem_limit_bytes=50 << 20
        ),
    )(tokens, routes.T, router_weights.T)
    return pl.pallas_call(
        widen,
        out_shape=jax.ShapeDtypeStruct((OWN, dev_rows, width), jnp.float32),
        in_specs=[pl.BlockSpec(memory_space=pltpu.VMEM)],
        out_specs=pl.BlockSpec(memory_space=pl.ANY),
        scratch_shapes=[pltpu.VMEM((OWN * dev_rows // STRIP, STRIP, width), jnp.float32), dma((OWN * dev_rows // STRIP,))],
        compiler_params=pltpu.CompilerParams(vmem_limit_bytes=16 << 20),
    )(blocks)


def solution(mesh):
    placed = (
        P(("expert", "panel"), None),
        P(("expert", "panel"), None),
        P(("expert", "panel"), None),
    )
    return jax.shard_map(
        per_device,
        mesh=mesh,
        in_specs=placed,
        out_specs=P("expert", "panel", None),
        check_vma=False,
    )
```
